32 devices in a mesh: groups: 1, row: 8 (over z, x), col: 4 (over y, core).
Axes of the slice: x: 2, y: 2, z: 4, core: 2. Of those that a mesh axis runs over, the one named last changes fastest.
Arguments:
- features: bfloat16 [512, 1536], P(('groups', 'row', 'col')), may hold values from -6 to 6
- first_weight: bfloat16 [1536, 48], replicated, may hold values from -0.15625 to 0.15625
- second_weight: bfloat16 [1536, 48], replicated, may hold values from -0.15625 to 0.15625
- conv_kernel: bfloat16 [3, 3, 48, 48], replicated, may hold values from -0.3125 to 0.3125
- conv_bias: float32 [48], replicated, may hold values from -3 to 3
- dilated_kernels: bfloat16 [3, 3, 3, 48, 48], replicated, may hold values from -0.3125 to 0.3125
- mixing_weights: bfloat16 [3, 48, 48], replicated, may hold values from -0.875 to 0.875
Outputs:
- contact_map: bfloat16 [48, 512, 512], P('groups', 'row', 'col')
The draws below stay inside these ranges and needn't reach their ends.
All inputs are finite; a program needn't handle non-finite values.
Results may differ from the reference program's by a relative error of at most 0.0065.
Values may be sent and summed in bfloat16 or wider, within the bound.
No kernel may reach another device: no remote copies, remote signals or barrier semaphores. Data moves between devices by JAX's collectives and lax.ppermute only.
A program may use at most 128 MiB of HBM per device.

```python
import jax
import jax.numpy as jnp
from jax import lax

C = 1536
CH = 48
BINS = 512


def block_levels(stream_key, shape, pieces, least, top_value):
    loudness, own = 1.0, jax.random.fold_in(stream_key, 6)
    for axis_at, blocks in pieces:
        steps = jnp.exp(jax.random.uniform(jax.random.fold_in(own, axis_at), (blocks,), jnp.float32, least / len(pieces), top_value / len(pieces)))
        loudness = loudness * jnp.repeat(steps, shape[axis_at] // blocks).reshape([-1 if axis == axis_at else 1 for axis in range(len(shape))])
    return loudness


def scatter_about(own_key, shape, scale, reach, cuts=(), kind=jnp.bfloat16):
    entries = scale * jax.random.normal(own_key, shape, jnp.float32)
    if cuts:
        entries = entries * block_levels(own_key, shape, cuts, -0.22, 0.18)
    return jnp.clip(entries, -reach, reach).astype(kind)


def setup_inputs(seed: int = 0, part: int = 0) -> dict:
    arg_keys = jax.random.split(jax.random.key(seed), 8)
    own_keys = jax.random.split(jax.random.fold_in(arg_keys[7], part), 8)
    features = scatter_about(own_keys[0], (BINS, C), 1.0, 6.0, ((0, 32),))
    first_weight = scatter_about(arg_keys[1], (C, CH), C ** -0.5, 0.15625)
    second_weight = scatter_about(arg_keys[2], (C, CH), C ** -0.5, 0.15625)
    conv_kernel = scatter_about(arg_keys[3], (3, 3, CH, CH), (9 * CH) ** -0.5, 0.3125)
    conv_bias = scatter_about(arg_keys[4], (CH,), 0.5, 3.0, (), jnp.float32)
    dilated_kernels = scatter_about(arg_keys[5], (3, 3, 3, CH, CH), (9 * CH) ** -0.5, 0.3125)
    mixing_weights = scatter_about(arg_keys[6], (3, CH, CH), CH ** -0.5, 0.875)
    return {"features": features, "first_weight": first_weight, "second_weight": second_weight, "conv_kernel": conv_kernel, "conv_bias": conv_bias, "dilated_kernels": dilated_kernels, "mixing_weights": mixing_weights}


def convolve(field, kernel, spread):
    weights = jnp.transpose(kernel.astype(jnp.float32), (2, 3, 0, 1))
    result = lax.conv_general_dilated(field.astype(jnp.float32)[None], weights, (1, 1), [(spread, spread), (spread, spread)], rhs_dilation=(spread, spread), dimension_numbers=("NCHW", "OIHW", "NCHW"), precision=lax.Precision.HIGHEST)
    return result[0]


def reference(features, first_weight, second_weight, conv_kernel, conv_bias, dilated_kernels, mixing_weights):
    proj_a = jnp.dot(features, first_weight, preferred_element_type=jnp.float32).astype(jnp.bfloat16)
    proj_b = jnp.dot(features, second_weight, preferred_element_type=jnp.float32).astype(jnp.bfloat16)
    grid = jax.nn.relu(proj_a.T.astype(jnp.float32)[:, :, None] + proj_b.T.astype(jnp.float32)[:, None, :]).astype(jnp.bfloat16)
    first = convolve(grid, conv_kernel, 1)
    state = 0.5 * (first + jnp.swapaxes(first, 1, 2)) + conv_bias[:, None, None]
    channels = state.shape[0]
    for block, spread in enumerate((2, 4, 8)):
        active = jax.nn.relu(state).astype(jnp.bfloat16)
        inner = convolve(active, dilated_kernels[block], spread)
        gated = jax.nn.relu(inner).astype(jnp.bfloat16)
        mixed = jnp.dot(mixing_weights[block], gated.reshape(channels, -1), preferred_element_type=jnp.float32)
        state = state + mixed.reshape(state.shape)
    return state.astype(jnp.bfloat16)
```

```python
import functools

import jax
import jax.numpy as jnp
from jax import lax
from jax.experimental import pallas as pl
from jax.experimental.pallas import tpu as pltpu
from jax.sharding import PartitionSpec as P

MARGIN = 16
GROUP = 8
LANES = 128
FAR = -1e30
SPREADS = (2, 4, 8)


def haloed(p_ref, start, count, bins):
    before = pl.multiple_of(jnp.maximum(start - MARGIN, 0), MARGIN)
    after = pl.multiple_of(jnp.minimum(start + count, bins - MARGIN), MARGIN)
    top = p_ref[pl.ds(before, MARGIN), :].astype(jnp.float32)
    mid = p_ref[pl.ds(pl.multiple_of(start, MARGIN), count), :].astype(jnp.float32)
    low = p_ref[pl.ds(after, MARGIN), :].astype(jnp.float32)
    top = jnp.where(start > 0, top, FAR)
    low = jnp.where(start + count < bins, low, FAR)
    return jnp.concatenate([top, mid, low], axis=0)


def trunk(
    rows_tile, cols_tile, bins, channels,
    pos_ref, p_ref, w1_ref, wd_ref, wm_ref, bias_ref, hi_ref, out_ref,
    rb, cpat, state, act, sq, sh, oscr,
):
    width = cols_tile + 2 * MARGIN
    height = rows_tile + 2 * MARGIN
    step = GROUP * width
    period = 4 * width
    tiles = period // LANES
    both = 2 * channels
    rows_t = jnp.transpose(haloed(p_ref, pos_ref[0], rows_tile, bins))
    cols_t = jnp.transpose(haloed(p_ref, pos_ref[1], cols_tile, bins))
    rb[0] = jnp.zeros((both, LANES), jnp.bfloat16)
    rb[height + 1] = jnp.zeros((both, LANES), jnp.bfloat16)
    for i in range(height):
        rb[i + 1] = jnp.broadcast_to(rows_t[:, i : i + 1], (both, LANES)).astype(jnp.bfloat16)
    cols_s = jnp.concatenate([cols_t[channels:], cols_t[:channels]], axis=0)
    cols_p = jnp.concatenate([cols_s] * 4, axis=1)
    for q in (-1, 0, 1):
        cpat[q + 1] = (pltpu.roll(cols_p, (-q) % period, axis=1) if q else cols_p).astype(jnp.bfloat16)

    lane = lax.broadcasted_iota(jnp.int32, (both, LANES), 1)
    bias = jnp.broadcast_to(bias_ref[...], (channels, 2 * LANES))
    zero = jnp.bfloat16(0)

    def clipped(value, off, size):
        hi = hi_ref[:, pl.ds(off, size)]
        hi = jnp.concatenate([hi] * (channels // 16), axis=0)
        return jnp.minimum(jnp.maximum(value, 0.0).astype(jnp.bfloat16), hi)

    def first(g, _):
        for pair in range(step // (2 * LANES)):
            halves = []
            for t in (2 * pair, 2 * pair + 1):
                base = 4 * (t // tiles)
                t = t % tiles
                r0 = (t * LANES) // width
                r1 = (t * LANES + LANES - 1) // width
                split = r1 * width - t * LANES
                pieces = []
                for p in (-1, 0, 1):
                    row = rb[g * GROUP + (base + r0 + p + 1)]
                    if r1 != r0:
                        row = jnp.where(lane < split, row, rb[g * GROUP + (base + r1 + p + 1)])
                    for q in (-1, 0, 1):
                        pieces.append(jnp.maximum(row + cpat[q + 1, :, t * LANES : (t + 1) * LANES], zero))
                halves.append(jnp.concatenate(pieces, axis=0))
            x = jnp.concatenate(halves, axis=1)
            off = pl.multiple_of(g * step + pair * 2 * LANES, LANES)
            st = 0.5 * jnp.dot(w1_ref[...], x, preferred_element_type=jnp.float32) + bias
            state[:, pl.ds(off, 2 * LANES)] = st
            act[:, pl.ds(off + LANES, 2 * LANES)] = clipped(st, off, 2 * LANES)
        return 0

    lax.fori_loop(0, height // GROUP, first, 0)

    edge = 0
    for block, spread in enumerate(SPREADS):
        shift = spread * width
        ragged = shift % LANES
        rest = (-shift) % LANES
        assert ragged == rest

        def spreadout(g, _, edge=edge, spread=spread, ragged=ragged):
            off = pl.multiple_of(g * step + edge * width, LANES)
            window = act[:, pl.ds(off, step + 2 * LANES)]
            for q in (-1, 0, 1):
                at = LANES + q * spread
                rows = slice((q + 1) * channels, (q + 2) * channels)
                sq[rows, pl.ds(off, step)] = window[:, at : at + step]
                if ragged:
                    at += ragged
                    sh[rows, pl.ds(off, step)] = window[:, at : at + step]
            return 0

        inner_rows = height - 2 * edge
        lax.fori_loop(0, inner_rows // GROUP, spreadout, 0)
        edge = 4 if spread == 2 else 2 * spread
        last = block == len(SPREADS) - 1
        side = sh if ragged else sq

        def dilated(g, _, edge=edge, block=block, shift=shift, ragged=ragged, side=side, last=last):
            outs = []
            for pair in range(step // (2 * LANES)):
                size = 2 * LANES
                off = pl.multiple_of(g * step + (edge * width + pair * size), LANES)
                x = jnp.concatenate(
                    [
                        side[:, pl.ds(pl.multiple_of(off - shift - ragged, LANES), size)],
                        sq[:, pl.ds(off, size)],
                        side[:, pl.ds(pl.multiple_of(off + shift - ragged, LANES), size)],
                    ],
                    axis=0,
                )
                inner = jnp.dot(wd_ref[block], x, preferred_element_type=jnp.float32)
                gated = jnp.maximum(inner, 0.0).astype(jnp.bfloat16)
                st = state[:, pl.ds(off, size)] + jnp.dot(
                    wm_ref[block], gated, preferred_element_type=jnp.float32
                )
                if last:
                    outs.append(st)
                else:
                    state[:, pl.ds(off, size)] = st
                    act[:, pl.ds(off + LANES, size)] = clipped(st, off, size)
            if last:
                whole = jnp.concatenate(outs, axis=1)
                for k in range(GROUP):
                    at = k * width + MARGIN
                    oscr[pl.ds(k, channels, stride=GROUP), :] = whole[:, at : at + LANES]
                rows = pl.ds(pl.multiple_of(g * GROUP, GROUP), GROUP)
                out_ref[:, rows, :] = oscr[...].reshape(channels, GROUP, LANES).astype(jnp.bfloat16)
            return 0

        lax.fori_loop(0, (height - 2 * edge) // GROUP, dilated, 0)


def local(
    features, first_weight, second_weight, conv_kernel, conv_bias, dilated_kernels, mixing_weights
):
    channels = first_weight.shape[1]
    row_count, col_count = lax.axis_size("row"), lax.axis_size("col")
    devices = row_count * col_count
    mine = jnp.concatenate(
        [
            jnp.dot(features, first_weight, preferred_element_type=jnp.float32),
            jnp.dot(features, second_weight, preferred_element_type=jnp.float32),
        ],
        1,
    ).astype(jnp.bfloat16)
    bins = features.shape[0] * devices
    both = lax.all_to_all(
        jnp.broadcast_to(mine[None], (devices,) + mine.shape), ("row", "col"), 0, 0
    ).reshape(bins, 2 * channels)
    rows_tile = bins // row_count
    cols_tile = bins // col_count
    height, width = rows_tile + 2 * MARGIN, cols_tile + 2 * MARGIN
    row_start = lax.axis_index("row") * rows_tile
    col_start = lax.axis_index("col") * cols_tile
    pos = jnp.stack([row_start, col_start]).astype(jnp.int32)
    row_ids = row_start - MARGIN + jnp.arange(height, dtype=jnp.int32)
    col_ids = col_start - MARGIN + jnp.arange(width, dtype=jnp.int32)
    inside = ((row_ids >= 0) & (row_ids < bins))[:, None] & ((col_ids >= 0) & (col_ids < bins))[None]
    hi = jnp.broadcast_to(
        jnp.where(inside, jnp.inf, 0.0).astype(jnp.bfloat16).reshape(1, height * width),
        (16, height * width),
    )
    straight = jnp.transpose(conv_kernel, (2, 0, 1, 3))
    swapped = jnp.transpose(conv_kernel, (2, 1, 0, 3))
    w1 = jnp.stack([straight, swapped], axis=3).reshape(channels, 18 * channels)
    wd = jnp.transpose(dilated_kernels, (0, 3, 1, 2, 4)).reshape(3, channels, 9 * channels)
    lanes = height * width
    vmem = pl.BlockSpec(memory_space=pltpu.VMEM)
    return pl.pallas_call(
        functools.partial(trunk, rows_tile, cols_tile, bins, channels),
        out_shape=jax.ShapeDtypeStruct((channels, rows_tile, cols_tile), jnp.bfloat16),
        in_specs=[pl.BlockSpec(memory_space=pltpu.SMEM)] + [vmem] * 6,
        out_specs=vmem,
        scratch_shapes=[
            pltpu.VMEM((height + 2, 2 * channels, LANES), jnp.bfloat16),
            pltpu.VMEM((3, 2 * channels, 4 * width), jnp.bfloat16),
            pltpu.VMEM((channels, lanes), jnp.float32),
            pltpu.VMEM((channels, lanes + 2 * LANES), jnp.bfloat16),
            pltpu.VMEM((3 * channels, lanes), jnp.bfloat16),
            pltpu.VMEM((3 * channels, lanes), jnp.bfloat16),
            pltpu.VMEM((channels * GROUP, LANES), jnp.float32),
        ],
        compiler_params=pltpu.CompilerParams(vmem_limit_bytes=56 << 20),
        name="trunk",
    )(pos, both, w1, wd, mixing_weights, conv_bias[:, None], hi)


def solution(mesh):
    in_specs = (P(("groups", "row", "col"), None), P(), P(), P(), P(), P(), P())
    out_specs = P("groups", "row", "col")
    return jax.shard_map(local, mesh=mesh, in_specs=in_specs, out_specs=out_specs, check_vma=False)
```

```python
import functools

import jax
import jax.numpy as jnp
from jax import lax
from jax.experimental import pallas as pl
from jax.experimental.pallas import tpu as pltpu
from jax.sharding import PartitionSpec as P

MARGIN = 16
GROUP = 16
LANES = 128
FAR = -1e30
SPREADS = (2, 4, 8)


def haloed(p_ref, start, count, bins):
    before = pl.multiple_of(jnp.maximum(start - MARGIN, 0), MARGIN)
    after = pl.multiple_of(jnp.minimum(start + count, bins - MARGIN), MARGIN)
    top = p_ref[pl.ds(before, MARGIN), :].astype(jnp.float32)
    mid = p_ref[pl.ds(pl.multiple_of(start, MARGIN), count), :].astype(jnp.float32)
    low = p_ref[pl.ds(after, MARGIN), :].astype(jnp.float32)
    top = jnp.where(start > 0, top, FAR)
    low = jnp.where(start + count < bins, low, FAR)
    return jnp.concatenate([top, mid, low], axis=0)


def trunk(
    rows_tile, cols_tile, bins, channels,
    pos_ref, p_ref, w1_ref, wd_ref, wm_ref, bias_ref, hi_ref, out_ref,
    rb, cpat, state, act_a, act_b, side, tail, oscr,
):
    width = cols_tile + 2 * MARGIN
    height = rows_tile + 2 * MARGIN
    period = 4 * width
    tiles = period // LANES
    both = 2 * channels
    rows_t = jnp.transpose(haloed(p_ref, pos_ref[0], rows_tile, bins))
    cols_t = jnp.transpose(haloed(p_ref, pos_ref[1], cols_tile, bins))
    rb[0] = jnp.zeros((both, LANES), jnp.bfloat16)
    rb[height + 1] = jnp.zeros((both, LANES), jnp.bfloat16)
    for i in range(height):
        rb[i + 1] = jnp.broadcast_to(rows_t[:, i : i + 1], (both, LANES)).astype(jnp.bfloat16)
    cols_s = jnp.concatenate([cols_t[channels:], cols_t[:channels]], axis=0)
    cpat[...] = jnp.concatenate([cols_s] * 4, axis=1).astype(jnp.bfloat16)

    lane = lax.broadcasted_iota(jnp.int32, (both, LANES), 1)
    half = lax.broadcasted_iota(jnp.int32, (channels, LANES), 1) < LANES // 2
    zero = jnp.bfloat16(0)

    def chunks(first_row, count, body):
        full = count // GROUP
        lax.fori_loop(0, full, lambda g, c: body(g * GROUP + first_row, GROUP) or c, 0)
        if count % GROUP:
            body(first_row + full * GROUP, count % GROUP)

    def clipped(value, off, size):
        return jnp.minimum(jnp.maximum(value, 0.0), hi_ref[:, pl.ds(off, size)]).astype(jnp.bfloat16)

    def gathered(z, spread):
        size = z.shape[1]
        return (
            z[channels : 2 * channels]
            + pltpu.roll(z[:channels], spread, axis=1)
            + pltpu.roll(z[2 * channels :], size - spread, axis=1)
        )

    def first(row0, rows):
        size = rows * width
        off = pl.multiple_of(row0 * width, LANES)
        zs = []
        for pair in range(size // (2 * LANES)):
            halves = []
            for t in (2 * pair, 2 * pair + 1):
                base = 4 * (t // tiles)
                t = t % tiles
                r0 = (t * LANES) // width
                r1 = (t * LANES + LANES - 1) // width
                split = r1 * width - t * LANES
                col = cpat[:, t * LANES : (t + 1) * LANES]
                pieces = []
                for p in (-1, 0, 1):
                    row = rb[row0 + (base + r0 + p + 1)]
                    if r1 != r0:
                        row = jnp.where(lane < split, row, rb[row0 + (base + r1 + p + 1)])
                    pieces.append(jnp.maximum(row + col, zero))
                halves.append(jnp.concatenate(pieces, axis=0))
            x = jnp.concatenate(halves, axis=1)
            zs.append(jnp.dot(w1_ref[...], x, preferred_element_type=jnp.float32))
        st = 0.5 * gathered(jnp.concatenate(zs, axis=1), 1) + bias_ref[...]
        act = clipped(st, off, size)
        turned = pltpu.roll(act.astype(jnp.float32), LANES // 2, axis=1).astype(jnp.bfloat16)
        ahead = jnp.where(half, tail[...], turned[:, :LANES])
        state[:, pl.ds(off, size)] = st
        act_a[:, pl.ds(off, size)] = act
        side[:, pl.ds(off, size)] = jnp.concatenate([ahead, turned[:, LANES:]], axis=1)
        tail[...] = turned[:, :LANES]

    tail[...] = jnp.zeros_like(tail)
    chunks(0, height, first)

    edge = 0
    src, dst = act_a, act_b
    for block, spread in enumerate(SPREADS):
        shift = spread * width
        ragged = shift % LANES
        assert ragged in (0, LANES // 2)
        edge = 4 if spread == 2 else 2 * spread
        last = block == len(SPREADS) - 1
        around = side if ragged else src

        def dilated(row0, rows, block=block, spread=spread, shift=shift, ragged=ragged, src=src, dst=dst,
                    around=around, last=last, edge=edge):
            size = rows * width
            off = pl.multiple_of(row0 * width, LANES)
            x = jnp.concatenate(
                [
                    around[:, pl.ds(pl.multiple_of(off - shift + ragged, LANES), size)],
                    src[:, pl.ds(off, size)],
                    around[:, pl.ds(pl.multiple_of(off + shift + ragged, LANES), size)],
                ],
                axis=0,
            )
            z = jnp.dot(wd_ref[block], x, preferred_element_type=jnp.float32)
            gated = jnp.maximum(gathered(z, spread), 0.0).astype(jnp.bfloat16)
            st = state[:, pl.ds(off, size)] + jnp.dot(
                wm_ref[block], gated, preferred_element_type=jnp.float32
            )
            if not last:
                state[:, pl.ds(off, size)] = st
                dst[:, pl.ds(off, size)] = clipped(st, off, size)
                return
            for k in range(rows):
                at = k * width + MARGIN
                oscr[pl.ds(k, channels, stride=GROUP), :] = st[:, at : at + LANES]
            place = pl.ds(pl.multiple_of(row0 - MARGIN, GROUP), GROUP)
            out_ref[:, place, :] = oscr[...].reshape(channels, GROUP, LANES).astype(jnp.bfloat16)

        chunks(edge, height - 2 * edge, dilated)
        src, dst = dst, src


def call_trunk(rows_tile, cols_tile, bins, channels, *operands):
    height, width = rows_tile + 2 * MARGIN, cols_tile + 2 * MARGIN
    lanes = height * width
    vmem = pl.BlockSpec(memory_space=pltpu.VMEM)
    return pl.pallas_call(
        functools.partial(trunk, rows_tile, cols_tile, bins, channels),
        out_shape=jax.ShapeDtypeStruct((channels, rows_tile, cols_tile), jnp.bfloat16),
        in_specs=[pl.BlockSpec(memory_space=pltpu.SMEM)] + [vmem] * 6,
        out_specs=vmem,
        scratch_shapes=[
            pltpu.VMEM((height + 2, 2 * channels, LANES), jnp.bfloat16),
            pltpu.VMEM((2 * channels, 4 * width), jnp.bfloat16),
            pltpu.VMEM((channels, lanes), jnp.float32),
            pltpu.VMEM((channels, lanes), jnp.bfloat16),
            pltpu.VMEM((channels, lanes), jnp.bfloat16),
            pltpu.VMEM((channels, lanes), jnp.bfloat16),
            pltpu.VMEM((channels, LANES), jnp.bfloat16),
            pltpu.VMEM((channels * GROUP, LANES), jnp.float32),
        ],
        compiler_params=pltpu.CompilerParams(vmem_limit_bytes=56 << 20),
        name="trunk",
    )(*operands)


def local(
    features, first_weight, second_weight, conv_kernel, conv_bias, dilated_kernels, mixing_weights
):
    channels = first_weight.shape[1]
    row_count, col_count = lax.axis_size("row"), lax.axis_size("col")
    devices = row_count * col_count
    mine = jnp.concatenate(
        [
            jnp.dot(features, first_weight, preferred_element_type=jnp.float32),
            jnp.dot(features, second_weight, preferred_element_type=jnp.float32),
        ],
        1,
    ).astype(jnp.bfloat16)
    bins = features.shape[0] * devices
    both = lax.all_to_all(
        jnp.broadcast_to(mine[None], (devices,) + mine.shape), ("row", "col"), 0, 0
    ).reshape(bins, 2 * channels)
    rows_tile = bins // row_count
    cols_tile = bins // col_count
    height, width = rows_tile + 2 * MARGIN, cols_tile + 2 * MARGIN
    row_start = lax.axis_index("row") * rows_tile
    col_start = lax.axis_index("col") * cols_tile
    pos = jnp.stack([row_start, col_start]).astype(jnp.int32)
    row_ids = row_start - MARGIN + jnp.arange(height, dtype=jnp.int32)
    col_ids = col_start - MARGIN + jnp.arange(width, dtype=jnp.int32)
    inside = ((row_ids >= 0) & (row_ids < bins))[:, None] & ((col_ids >= 0) & (col_ids < bins))[None]
    hi = jnp.where(inside, jnp.inf, 0.0).astype(jnp.float32).reshape(1, height * width)
    straight = jnp.transpose(conv_kernel, (1, 2, 0, 3))
    swapped = jnp.transpose(conv_kernel, (0, 2, 1, 3))
    w1 = jnp.stack([straight, swapped], axis=3).reshape(3 * channels, 6 * channels)
    wd = jnp.transpose(dilated_kernels, (0, 2, 3, 1, 4)).reshape(3, 3 * channels, 3 * channels)
    return call_trunk(
        rows_tile, cols_tile, bins, channels, pos, both, w1, wd, mixing_weights, conv_bias[:, None], hi
    )


def solution(mesh):
    in_specs = (P(("groups", "row", "col"), None), P(), P(), P(), P(), P(), P())
    out_specs = P("groups", "row", "col")
    return jax.shard_map(local, mesh=mesh, in_specs=in_specs, out_specs=out_specs, check_vma=False)
```

```python
import functools

import jax
import jax.numpy as jnp
from jax import lax
from jax.experimental import pallas as pl
from jax.experimental.pallas import tpu as pltpu
from jax.sharding import PartitionSpec as P

MARGIN = 16
GROUP = 16
LANES = 128
FAR = -1e30
SPREADS = (2, 4, 8)


def haloed(p_ref, start, count, bins):
    before = pl.multiple_of(jnp.maximum(start - MARGIN, 0), MARGIN)
    after = pl.multiple_of(jnp.minimum(start + count, bins - MARGIN), MARGIN)
    top = p_ref[pl.ds(before, MARGIN), :].astype(jnp.float32)
    mid = p_ref[pl.ds(pl.multiple_of(start, MARGIN), count), :].astype(jnp.float32)
    low = p_ref[pl.ds(after, MARGIN), :].astype(jnp.float32)
    top = jnp.where(start > 0, top, FAR)
    low = jnp.where(start + count < bins, low, FAR)
    return jnp.concatenate([top, mid, low], axis=0)


def trunk(
    rows_tile, cols_tile, bins, channels,
    pos_ref, p_ref, w1_ref, wd_ref, wm_ref, bias_ref, hi_ref, out_ref,
):
    height, width = rows_tile + 2 * MARGIN, cols_tile + 2 * MARGIN
    lanes = height * width
    both = 2 * channels
    z_shape = pltpu.VMEM((3 * channels, GROUP * width), jnp.float32)
    pl.run_scoped(
        functools.partial(
            staged, rows_tile, cols_tile, bins, channels,
            pos_ref, p_ref, w1_ref, wd_ref, wm_ref, bias_ref, hi_ref, out_ref,
        ),
        pltpu.VMEM((height + 2, both, LANES), jnp.bfloat16),
        pltpu.VMEM((both, 4 * width), jnp.bfloat16),
        pltpu.VMEM((channels, lanes), jnp.float32),
        pltpu.VMEM((channels, lanes), jnp.bfloat16),
        pltpu.VMEM((channels, lanes), jnp.bfloat16),
        pltpu.VMEM((channels, lanes), jnp.bfloat16),
        pltpu.VMEM((channels, LANES), jnp.bfloat16),
        pltpu.VMEM((channels * GROUP, LANES), jnp.float32),
        z_shape,
        z_shape,
    )


def staged(
    rows_tile, cols_tile, bins, channels,
    pos_ref, p_ref, w1_ref, wd_ref, wm_ref, bias_ref, hi_ref, out_ref,
    rb, cpat, state, act_a, act_b, side, tail, oscr, z_a, z_b,
):
    width = cols_tile + 2 * MARGIN
    height = rows_tile + 2 * MARGIN
    period = 4 * width
    tiles = period // LANES
    both = 2 * channels
    zero = jnp.bfloat16(0)
    rows_t = jnp.transpose(haloed(p_ref, pos_ref[0], rows_tile, bins)).astype(jnp.bfloat16)
    cols_t = jnp.transpose(haloed(p_ref, pos_ref[1], cols_tile, bins))
    rb[0] = jnp.zeros((both, LANES), jnp.bfloat16)
    rb[height + 1] = jnp.zeros((both, LANES), jnp.bfloat16)
    for i in range(height):
        rb[i + 1] = jnp.broadcast_to(rows_t[:, i : i + 1], (both, LANES))
    cols_s = jnp.concatenate([cols_t[channels:], cols_t[:channels]], axis=0)
    cpat[...] = jnp.concatenate([cols_s] * 4, axis=1).astype(jnp.bfloat16)
    tail[...] = jnp.zeros_like(tail)

    lane = lax.broadcasted_iota(jnp.int32, (both, LANES), 1)

    def at(row0, rows, shift=0):
        start = row0 * width + shift
        return pl.ds(start if isinstance(start, int) else pl.multiple_of(start, LANES), rows * width)

    def gathered(z_ref, rows, spread):
        size = rows * width
        return (
            z_ref[channels : 2 * channels, :size]
            + pltpu.roll(z_ref[:channels, :size], spread, axis=1)
            + pltpu.roll(z_ref[2 * channels :, :size], size - spread, axis=1)
        )

    def grid_part(row0, rows, z_ref):
        size = rows * width
        for pair in range(size // (2 * LANES)):
            halves = []
            for t in (2 * pair, 2 * pair + 1):
                base = 4 * (t // tiles)
                t = t % tiles
                r0 = (t * LANES) // width
                r1 = (t * LANES + LANES - 1) // width
                split = r1 * width - t * LANES
                col = cpat[:, t * LANES : (t + 1) * LANES]
                pieces = []
                for p in (-1, 0, 1):
                    row = rb[row0 + (base + r0 + p + 1)]
                    if r1 != r0:
                        row = jnp.where(lane < split, row, rb[row0 + (base + r1 + p + 1)])
                    pieces.append(jnp.maximum(row + col, zero))
                halves.append(jnp.concatenate(pieces, axis=0))
            x = jnp.concatenate(halves, axis=1)
            z_ref[:, pair * 2 * LANES : (pair + 1) * 2 * LANES] = jnp.dot(
                w1_ref[...], x, preferred_element_type=jnp.float32
            )

    def start_part(row0, rows, z_ref):
        size = rows * width
        st = jnp.minimum(gathered(z_ref, rows, 1) + bias_ref[...], hi_ref[:, at(row0, rows)])
        act = jnp.maximum(st.astype(jnp.bfloat16), zero)
        window = jnp.concatenate([tail[...], act], axis=1)
        tail[...] = act[:, size - LANES :]
        state[:, at(row0, rows)] = st
        act_a[:, at(row0, rows)] = act
        side[:, at(row0, rows)] = window[:, LANES // 2 : LANES // 2 + size]

    stages = [(0, height, grid_part, start_part)]
    src, dst = act_a, act_b
    for block, spread in enumerate(SPREADS):
        shift = spread * width
        ragged = shift % LANES
        assert ragged in (0, LANES // 2)
        edge = 4 if spread == 2 else 2 * spread
        last = block == len(SPREADS) - 1
        around = side if ragged else src

        def conv_part(row0, rows, z_ref, block=block, shift=shift, ragged=ragged, src=src, around=around):
            x = jnp.concatenate(
                [
                    around[:, at(row0, rows, ragged - shift)],
                    src[:, at(row0, rows)],
                    around[:, at(row0, rows, ragged + shift)],
                ],
                axis=0,
            )
            z_ref[:, : rows * width] = jnp.dot(wd_ref[block], x, preferred_element_type=jnp.float32)

        def mix_part(row0, rows, z_ref, block=block, spread=spread, dst=dst, last=last):
            gated = jnp.maximum(gathered(z_ref, rows, spread).astype(jnp.bfloat16), zero)
            st = state[:, at(row0, rows)] + jnp.dot(wm_ref[block], gated, preferred_element_type=jnp.float32)
            if not last:
                state[:, at(row0, rows)] = st
                dst[:, at(row0, rows)] = jnp.maximum(st.astype(jnp.bfloat16), zero)
                return
            for k in range(rows):
                oscr[pl.ds(k, channels, stride=GROUP), :] = st[:, k * width + MARGIN : k * width + MARGIN + LANES]
            start = row0 - MARGIN
            place = pl.ds(start if isinstance(start, int) else pl.multiple_of(start, GROUP), GROUP)
            out_ref[:, place, :] = oscr[...].reshape(channels, GROUP, LANES).astype(jnp.bfloat16)

        stages.append((edge, height - 2 * edge, conv_part, mix_part))
        src, dst = dst, src

    slots = (z_a, z_b)
    waiting = None
    turn = 0
    for first_row, count, before, after in stages:
        groups = count // GROUP
        before(first_row, GROUP, slots[turn])
        if waiting is not None:
            waiting()

        def body(h, carry, first_row=first_row, before=before, after=after, turn=turn):
            row0 = first_row + h * (2 * GROUP)
            before(row0 + GROUP, GROUP, slots[1 - turn])
            after(row0, GROUP, slots[turn])
            before(row0 + 2 * GROUP, GROUP, slots[turn])
            after(row0 + GROUP, GROUP, slots[1 - turn])
            return carry

        lax.fori_loop(0, (groups - 1) // 2, body, 0)
        row0 = first_row + (groups - 1) // 2 * (2 * GROUP)
        sizes = [GROUP] * ((groups - 1) % 2) + [count % GROUP] * (count % GROUP > 0)
        size = GROUP
        for following in sizes:
            before(row0 + size, following, slots[1 - turn])
            after(row0, size, slots[turn])
            row0, size, turn = row0 + size, following, 1 - turn
        waiting = functools.partial(after, row0, size, slots[turn])
        turn = 1 - turn
    waiting()


def call_trunk(rows_tile, cols_tile, bins, channels, *operands):
    vmem = pl.BlockSpec(memory_space=pltpu.VMEM)
    return pl.pallas_call(
        functools.partial(trunk, rows_tile, cols_tile, bins, channels),
        out_shape=jax.ShapeDtypeStruct((channels, rows_tile, cols_tile), jnp.bfloat16),
        in_specs=[pl.BlockSpec(memory_space=pltpu.SMEM)] + [vmem] * 6,
        out_specs=vmem,
        compiler_params=pltpu.CompilerParams(vmem_limit_bytes=56 << 20),
        name="trunk",
    )(*operands)


def local(
    features, first_weight, second_weight, conv_kernel, conv_bias, dilated_kernels, mixing_weights
):
    channels = first_weight.shape[1]
    row_count, col_count = lax.axis_size("row"), lax.axis_size("col")
    devices = row_count * col_count
    mine = jnp.concatenate(
        [
            jnp.dot(features, first_weight, preferred_element_type=jnp.float32),
            jnp.dot(features, second_weight, preferred_element_type=jnp.float32),
        ],
        1,
    ).astype(jnp.bfloat16)
    bins = features.shape[0] * devices
    both = lax.all_to_all(
        jnp.broadcast_to(mine[None], (devices,) + mine.shape), ("row", "col"), 0, 0
    ).reshape(bins, 2 * channels)
    rows_tile = bins // row_count
    cols_tile = bins // col_count
    height, width = rows_tile + 2 * MARGIN, cols_tile + 2 * MARGIN
    row_start = lax.axis_index("row") * rows_tile
    col_start = lax.axis_index("col") * cols_tile
    pos = jnp.stack([row_start, col_start]).astype(jnp.int32)
    row_ids = row_start - MARGIN + jnp.arange(height, dtype=jnp.int32)
    col_ids = col_start - MARGIN + jnp.arange(width, dtype=jnp.int32)
    inside = ((row_ids >= 0) & (row_ids < bins))[:, None] & ((col_ids >= 0) & (col_ids < bins))[None]
    hi = jnp.where(inside, jnp.inf, FAR).astype(jnp.float32).reshape(1, height * width)
    straight = jnp.transpose(conv_kernel, (1, 2, 0, 3))
    swapped = jnp.transpose(conv_kernel, (0, 2, 1, 3))
    w1 = (0.5 * jnp.stack([straight, swapped], axis=3)).astype(jnp.bfloat16).reshape(3 * channels, 6 * channels)
    wd = jnp.transpose(dilated_kernels, (0, 2, 3, 1, 4)).reshape(3, 3 * channels, 3 * channels)
    return call_trunk(
        rows_tile, cols_tile, bins, channels, pos, both, w1, wd, mixing_weights, conv_bias[:, None], hi
    )


def solution(mesh):
    in_specs = (P(("groups", "row", "col"), None), P(), P(), P(), P(), P(), P())
    out_specs = P("groups", "row", "col")
    return jax.shard_map(local, mesh=mesh, in_specs=in_specs, out_specs=out_specs, check_vma=False)
```

```python
import functools

import jax
import jax.numpy as jnp
from jax import lax
from jax.experimental import pallas as pl
from jax.experimental.pallas import tpu as pltpu
from jax.sharding import PartitionSpec as P

MARGIN = 16
GROUP = 16
LANES = 128
FAR = -1e30
SPREADS = (2, 4, 8)


def haloed(p_ref, start, count, bins):
    before = pl.multiple_of(jnp.maximum(start - MARGIN, 0), MARGIN)
    after = pl.multiple_of(jnp.minimum(start + count, bins - MARGIN), MARGIN)
    top = p_ref[pl.ds(before, MARGIN), :].astype(jnp.float32)
    mid = p_ref[pl.ds(pl.multiple_of(start, MARGIN), count), :].astype(jnp.float32)
    low = p_ref[pl.ds(after, MARGIN), :].astype(jnp.float32)
    top = jnp.where(start > 0, top, FAR)
    low = jnp.where(start + count < bins, low, FAR)
    return jnp.concatenate([top, mid, low], axis=0)


def trunk(
    rows_tile, cols_tile, bins, channels,
    pos_ref, p_ref, w1_ref, wd_ref, wm_ref, bias_ref, hi_ref, out_ref,
):
    height, width = rows_tile + 2 * MARGIN, cols_tile + 2 * MARGIN
    lanes = height * width
    both = 2 * channels
    z_shape = pltpu.VMEM((3 * channels, GROUP * width), jnp.float32)
    pl.run_scoped(
        functools.partial(
            staged, rows_tile, cols_tile, bins, channels,
            pos_ref, p_ref, w1_ref, wd_ref, wm_ref, bias_ref, hi_ref, out_ref,
        ),
        pltpu.VMEM((height + 2, both, LANES), jnp.bfloat16),
        pltpu.VMEM((both, 4 * width), jnp.bfloat16),
        pltpu.VMEM((channels, lanes), jnp.float32),
        pltpu.VMEM((channels, lanes), jnp.bfloat16),
        pltpu.VMEM((channels, lanes), jnp.bfloat16),
        pltpu.VMEM((channels, lanes), jnp.bfloat16),
        pltpu.VMEM((channels, LANES), jnp.bfloat16),
        pltpu.VMEM((channels * GROUP, LANES), jnp.float32),
        z_shape,
        z_shape,
    )


def staged(
    rows_tile, cols_tile, bins, channels,
    pos_ref, p_ref, w1_ref, wd_ref, wm_ref, bias_ref, hi_ref, out_ref,
    rb, cpat, state, act_a, act_b, side, tail, oscr, z_a, z_b,
):
    width = cols_tile + 2 * MARGIN
    height = rows_tile + 2 * MARGIN
    period = 4 * width
    tiles = period // LANES
    both = 2 * channels
    zero = jnp.bfloat16(0)
    rows_t = jnp.transpose(haloed(p_ref, pos_ref[0], rows_tile, bins)).astype(jnp.bfloat16)
    cols_t = jnp.transpose(haloed(p_ref, pos_ref[1], cols_tile, bins))
    rb[0] = jnp.zeros((both, LANES), jnp.bfloat16)
    rb[height + 1] = jnp.zeros((both, LANES), jnp.bfloat16)
    for i in range(height):
        rb[i + 1] = jnp.broadcast_to(rows_t[:, i : i + 1], (both, LANES))
    cols_s = jnp.concatenate([cols_t[channels:], cols_t[:channels]], axis=0)
    cpat[...] = jnp.concatenate([cols_s] * 4, axis=1).astype(jnp.bfloat16)
    tail[...] = jnp.zeros_like(tail)

    lane = lax.broadcasted_iota(jnp.int32, (both, LANES), 1)

    def at(row0, rows, shift=0):
        start = row0 * width + shift
        return pl.ds(start if isinstance(start, int) else pl.multiple_of(start, LANES), rows * width)

    def gathered(z_ref, rows, spread):
        size = rows * width
        return (
            z_ref[channels : 2 * channels, :size]
            + pltpu.roll(z_ref[:channels, :size], spread, axis=1)
            + pltpu.roll(z_ref[2 * channels :, :size], size - spread, axis=1)
        )

    def grid_part(row0, rows, z_ref):
        size = rows * width
        for pair in range(size // (2 * LANES)):
            halves = []
            for t in (2 * pair, 2 * pair + 1):
                base = 4 * (t // tiles)
                t = t % tiles
                r0 = (t * LANES) // width
                r1 = (t * LANES + LANES - 1) // width
                split = r1 * width - t * LANES
                col = cpat[:, t * LANES : (t + 1) * LANES]
                pieces = []
                for p in (-1, 0, 1):
                    row = rb[row0 + (base + r0 + p + 1)]
                    if r1 != r0:
                        row = jnp.where(lane < split, row, rb[row0 + (base + r1 + p + 1)])
                    pieces.append(jnp.maximum(row + col, zero))
                halves.append(jnp.concatenate(pieces, axis=0))
            x = jnp.concatenate(halves, axis=1)
            z_ref[:, pair * 2 * LANES : (pair + 1) * 2 * LANES] = jnp.dot(
                w1_ref[...], x, preferred_element_type=jnp.float32
            )

    def start_part(row0, rows, z_ref):
        size = rows * width
        st = jnp.minimum(gathered(z_ref, rows, 1) + bias_ref[...], hi_ref[:, at(row0, rows)])
        act = jnp.maximum(st.astype(jnp.bfloat16), zero)
        window = jnp.concatenate([tail[...], act], axis=1)
        tail[...] = act[:, size - LANES :]
        state[:, at(row0, rows)] = st
        act_a[:, at(row0, rows)] = act
        side[:, at(row0, rows)] = window[:, LANES // 2 : LANES // 2 + size]

    stages = [(0, height, grid_part, start_part)]
    src, dst = act_a, act_b
    for block, spread in enumerate(SPREADS):
        shift = spread * width
        ragged = shift % LANES
        assert ragged in (0, LANES // 2)
        edge = 4 if spread == 2 else 2 * spread
        last = block == len(SPREADS) - 1
        around = side if ragged else src

        def conv_part(row0, rows, z_ref, block=block, shift=shift, ragged=ragged, src=src, around=around):
            x = jnp.concatenate(
                [
                    around[:, at(row0, rows, ragged - shift)],
                    src[:, at(row0, rows)],
                    around[:, at(row0, rows, ragged + shift)],
                ],
                axis=0,
            )
            z_ref[:, : rows * width] = jnp.dot(wd_ref[block], x, preferred_element_type=jnp.float32)

        def mix_part(row0, rows, z_ref, block=block, spread=spread, dst=dst, last=last):
            gated = jnp.maximum(gathered(z_ref, rows, spread).astype(jnp.bfloat16), zero)
            st = state[:, at(row0, rows)] + jnp.dot(wm_ref[block], gated, preferred_element_type=jnp.float32)
            if not last:
                state[:, at(row0, rows)] = st
                dst[:, at(row0, rows)] = jnp.maximum(st.astype(jnp.bfloat16), zero)
                return
            for k in range(rows):
                oscr[pl.ds(k, channels, stride=GROUP), :] = st[:, k * width + MARGIN : k * width + MARGIN + LANES]
            start = row0 - MARGIN
            place = pl.ds(start if isinstance(start, int) else pl.multiple_of(start, GROUP), GROUP)
            out_ref[:, place, :] = oscr[...].reshape(channels, GROUP, LANES).astype(jnp.bfloat16)

        stages.append((edge, height - 2 * edge, conv_part, mix_part))
        src, dst = dst, src

    slots = (z_a, z_b)
    waiting = None
    turn = 0
    for first_row, count, before, after in stages:
        groups = count // GROUP
        before(first_row, GROUP, slots[turn])
        if waiting is not None:
            waiting()

        def body(h, carry, first_row=first_row, before=before, after=after, turn=turn):
            row0 = first_row + h * (2 * GROUP)
            before(row0 + GROUP, GROUP, slots[1 - turn])
            after(row0, GROUP, slots[turn])
            before(row0 + 2 * GROUP, GROUP, slots[turn])
            after(row0 + GROUP, GROUP, slots[1 - turn])
            return carry

        lax.fori_loop(0, (groups - 1) // 2, body, 0)
        row0 = first_row + (groups - 1) // 2 * (2 * GROUP)
        sizes = [GROUP] * ((groups - 1) % 2) + [count % GROUP] * (count % GROUP > 0)
        size = GROUP
        for following in sizes:
            before(row0 + size, following, slots[1 - turn])
            after(row0, size, slots[turn])
            row0, size, turn = row0 + size, following, 1 - turn
        waiting = functools.partial(after, row0, size, slots[turn])
        turn = 1 - turn
    waiting()


def project(count, f_ref, first_ref, second_ref, out_ref):
    weights = jnp.concatenate([first_ref[...], second_ref[...]], axis=0)
    mine = lax.dot_general(
        f_ref[...], weights, (((1,), (1,)), ((), ())), preferred_element_type=jnp.float32
    ).astype(jnp.bfloat16)
    out_ref[...] = jnp.broadcast_to(mine[None], (count,) + mine.shape)


def vmem_need(rows_tile, cols_tile, channels):
    height, width = rows_tile + 2 * MARGIN, cols_tile + 2 * MARGIN
    lanes = height * width
    cells = lanes * channels
    sums = 2 * 3 * channels * GROUP * width * 4
    grid = (height + 2) * 2 * channels * LANES * 2
    return cells * 4 + 3 * cells * 2 + sums + grid + channels * rows_tile * LANES * 2 + (6 << 20)


def call_trunk(rows_tile, cols_tile, bins, channels, *operands):
    vmem = pl.BlockSpec(memory_space=pltpu.VMEM)
    return pl.pallas_call(
        functools.partial(trunk, rows_tile, cols_tile, bins, channels),
        out_shape=jax.ShapeDtypeStruct((channels, rows_tile, cols_tile), jnp.bfloat16),
        in_specs=[pl.BlockSpec(memory_space=pltpu.SMEM)] + [vmem] * 6,
        out_specs=vmem,
        compiler_params=pltpu.CompilerParams(vmem_limit_bytes=vmem_need(rows_tile, cols_tile, channels)),
        name="trunk",
    )(*operands)


def local(
    features, first_weight, second_weight, conv_kernel, conv_bias, dilated_kernels, mixing_weights
):
    channels = first_weight.shape[1]
    row_count, col_count = lax.axis_size("row"), lax.axis_size("col")
    devices = row_count * col_count
    bins = features.shape[0] * devices
    vmem = pl.BlockSpec(memory_space=pltpu.VMEM)
    copies = pl.pallas_call(
        functools.partial(project, devices),
        out_shape=jax.ShapeDtypeStruct((devices, features.shape[0], 2 * channels), jnp.bfloat16),
        in_specs=[vmem] * 3,
        out_specs=vmem,
        compiler_params=pltpu.CompilerParams(vmem_limit_bytes=60 << 20),
        name="project",
    )(features, first_weight.T, second_weight.T)
    both = lax.all_to_all(copies, ("row", "col"), 0, 0).reshape(bins, 2 * channels)
    rows_tile = bins // row_count
    cols_tile = bins // col_count
    height, width = rows_tile + 2 * MARGIN, cols_tile + 2 * MARGIN
    row_start = lax.axis_index("row") * rows_tile
    col_start = lax.axis_index("col") * cols_tile
    pos = jnp.stack([row_start, col_start]).astype(jnp.int32)
    row_ids = row_start - MARGIN + jnp.arange(height, dtype=jnp.int32)
    col_ids = col_start - MARGIN + jnp.arange(width, dtype=jnp.int32)
    inside = ((row_ids >= 0) & (row_ids < bins))[:, None] & ((col_ids >= 0) & (col_ids < bins))[None]
    hi = jnp.where(inside, jnp.inf, FAR).astype(jnp.float32).reshape(1, height * width)
    straight = jnp.transpose(conv_kernel, (1, 2, 0, 3))
    swapped = jnp.transpose(conv_kernel, (0, 2, 1, 3))
    w1 = (0.5 * jnp.stack([straight, swapped], axis=3)).astype(jnp.bfloat16).reshape(3 * channels, 6 * channels)
    wd = jnp.transpose(dilated_kernels, (0, 2, 3, 1, 4)).reshape(3, 3 * channels, 3 * channels)
    return call_trunk(
        rows_tile, cols_tile, bins, channels, pos, both, w1, wd, mixing_weights, conv_bias[:, None], hi
    )


def solution(mesh):
    in_specs = (P(("groups", "row", "col"), None), P(), P(), P(), P(), P(), P())
    out_specs = P("groups", "row", "col")
    return jax.shard_map(local, mesh=mesh, in_specs=in_specs, out_specs=out_specs, check_vma=False)
```

```python
import functools

import jax
import jax.numpy as jnp
from jax import lax
from jax.experimental import pallas as pl
from jax.experimental.pallas import tpu as pltpu
from jax.sharding import PartitionSpec as P

MARGIN = 16
GROUP = 16
LANES = 128
FAR = -1e30
SPREADS = (2, 4, 8)


def haloed(p_ref, start, count, bins):
    before = pl.multiple_of(jnp.maximum(start - MARGIN, 0), MARGIN)
    after = pl.multiple_of(jnp.minimum(start + count, bins - MARGIN), MARGIN)
    top = p_ref[pl.ds(before, MARGIN), :].astype(jnp.float32)
    mid = p_ref[pl.ds(pl.multiple_of(start, MARGIN), count), :].astype(jnp.float32)
    low = p_ref[pl.ds(after, MARGIN), :].astype(jnp.float32)
    top = jnp.where(start > 0, top, FAR)
    low = jnp.where(start + count < bins, low, FAR)
    return jnp.concatenate([top, mid, low], axis=0)


def trunk(
    rows_tile, cols_tile, bins, channels,
    pos_ref, p_ref, w1_ref, wd_ref, wm_ref, bias_ref, hi_ref, out_ref, staging, sems,
):
    height, width = rows_tile + 2 * MARGIN, cols_tile + 2 * MARGIN
    lanes = height * width
    both = 2 * channels
    z_shape = pltpu.VMEM((3 * channels, GROUP * width), jnp.float32)
    pl.run_scoped(
        functools.partial(
            staged, rows_tile, cols_tile, bins, channels,
            pos_ref, p_ref, w1_ref, wd_ref, wm_ref, bias_ref, hi_ref, out_ref, staging, sems,
        ),
        pltpu.VMEM((height + 2, both, LANES), jnp.bfloat16),
        pltpu.VMEM((both, 4 * width), jnp.bfloat16),
        pltpu.VMEM((channels, lanes), jnp.float32),
        pltpu.VMEM((channels, lanes), jnp.bfloat16),
        pltpu.VMEM((channels, lanes), jnp.bfloat16),
        pltpu.VMEM((channels, lanes), jnp.bfloat16),
        pltpu.VMEM((channels, LANES), jnp.bfloat16),
        pltpu.VMEM((channels * GROUP, LANES), jnp.float32),
        pltpu.VMEM((channels * GROUP, LANES), jnp.float32),
        z_shape,
        z_shape,
    )


def staged(
    rows_tile, cols_tile, bins, channels,
    pos_ref, p_ref, w1_ref, wd_ref, wm_ref, bias_ref, hi_ref, out_ref, staging, sems,
    rb, cpat, state, act_a, act_b, side, tail, flat_a, flat_b, z_a, z_b,
):
    width = cols_tile + 2 * MARGIN
    height = rows_tile + 2 * MARGIN
    period = 4 * width
    tiles = period // LANES
    both = 2 * channels
    zero = jnp.bfloat16(0)
    rows_t = jnp.transpose(haloed(p_ref, pos_ref[0], rows_tile, bins)).astype(jnp.bfloat16)
    cols_t = jnp.transpose(haloed(p_ref, pos_ref[1], cols_tile, bins))
    rb[0] = jnp.zeros((both, LANES), jnp.bfloat16)
    rb[height + 1] = jnp.zeros((both, LANES), jnp.bfloat16)
    ready = set()

    def prepare(start, stop):
        for i in range(max(start, 0), min(stop, height)):
            if i not in ready:
                ready.add(i)
                rb[i + 1] = jnp.broadcast_to(rows_t[:, i : i + 1], (both, LANES))

    cols_s = jnp.concatenate([cols_t[channels:], cols_t[:channels]], axis=0)
    cpat[...] = jnp.concatenate([cols_s] * 4, axis=1).astype(jnp.bfloat16)
    tail[...] = jnp.zeros_like(tail)

    lane = lax.broadcasted_iota(jnp.int32, (both, LANES), 1)

    def at(row0, rows, shift=0):
        start = row0 * width + shift
        return pl.ds(start if isinstance(start, int) else pl.multiple_of(start, LANES), rows * width)

    def gathered(z_ref, rows, spread):
        size = rows * width
        return (
            z_ref[channels : 2 * channels, :size]
            + pltpu.roll(z_ref[:channels, :size], spread, axis=1)
            + pltpu.roll(z_ref[2 * channels :, :size], size - spread, axis=1)
        )

    def grid_part(row0, rows, z_ref):
        size = rows * width
        if isinstance(row0, int):
            prepare(row0 - 1, row0 + rows + 1)
        for pair in range(size // (2 * LANES)):
            halves = []
            for t in (2 * pair, 2 * pair + 1):
                base = 4 * (t // tiles)
                t = t % tiles
                r0 = (t * LANES) // width
                r1 = (t * LANES + LANES - 1) // width
                split = r1 * width - t * LANES
                col = cpat[:, t * LANES : (t + 1) * LANES]
                pieces = []
                for p in (-1, 0, 1):
                    row = rb[row0 + (base + r0 + p + 1)]
                    if r1 != r0:
                        row = jnp.where(lane < split, row, rb[row0 + (base + r1 + p + 1)])
                    pieces.append(jnp.maximum(row + col, zero))
                halves.append(jnp.concatenate(pieces, axis=0))
            x = jnp.concatenate(halves, axis=1)
            z_ref[:, pair * 2 * LANES : (pair + 1) * 2 * LANES] = jnp.dot(
                w1_ref[...], x, preferred_element_type=jnp.float32
            )

    def start_part(row0, rows, z_ref):
        size = rows * width
        st = jnp.minimum(gathered(z_ref, rows, 1) + bias_ref[...], hi_ref[:, at(row0, rows)])
        act = jnp.maximum(st.astype(jnp.bfloat16), zero)
        window = jnp.concatenate([tail[...], act], axis=1)
        tail[...] = act[:, size - LANES :]
        state[:, at(row0, rows)] = st
        act_a[:, at(row0, rows)] = act
        side[:, at(row0, rows)] = window[:, LANES // 2 : LANES // 2 + size]

    stages = [(0, height, grid_part, start_part)]
    src, dst = act_a, act_b
    for block, spread in enumerate(SPREADS):
        shift = spread * width
        ragged = shift % LANES
        assert ragged in (0, LANES // 2)
        edge = 4 if spread == 2 else 2 * spread
        last = block == len(SPREADS) - 1
        around = side if ragged else src

        def conv_part(row0, rows, z_ref, block=block, shift=shift, ragged=ragged, src=src, around=around):
            x = jnp.concatenate(
                [
                    around[:, at(row0, rows, ragged - shift)],
                    src[:, at(row0, rows)],
                    around[:, at(row0, rows, ragged + shift)],
                ],
                axis=0,
            )
            z_ref[:, : rows * width] = jnp.dot(wd_ref[block], x, preferred_element_type=jnp.float32)

        def mix_part(row0, rows, z_ref, block=block, spread=spread, dst=dst, last=last):
            gated = jnp.maximum(gathered(z_ref, rows, spread).astype(jnp.bfloat16), zero)
            st = state[:, at(row0, rows)] + jnp.dot(wm_ref[block], gated, preferred_element_type=jnp.float32)
            flat = flat_a if z_ref is z_a else flat_b
            if not last:
                state[:, at(row0, rows)] = st
                dst[:, at(row0, rows)] = jnp.maximum(st.astype(jnp.bfloat16), zero)
                return
            st = st.astype(jnp.bfloat16)
            for k in range(rows):
                row = st[:, k * width + MARGIN : k * width + MARGIN + LANES]
                flat[pl.ds(k, channels, stride=GROUP), :] = row.astype(jnp.float32)
            start = row0 - MARGIN
            place = pl.ds(start if isinstance(start, int) else pl.multiple_of(start, GROUP), GROUP)
            staging[:, place, :] = flat[...].reshape(channels, GROUP, LANES).astype(jnp.bfloat16)
            sent(start).start()

        stages.append((edge, height - 2 * edge, conv_part, mix_part))
        src, dst = dst, src

    def sent(start):
        place = pl.ds(start if isinstance(start, int) else pl.multiple_of(start, GROUP), GROUP)
        return pltpu.make_async_copy(staging.at[:, place, :], out_ref.at[:, place, :], sems.at[start // GROUP])

    slots = (z_a, z_b)
    waiting = None
    turn = 0
    for first_row, count, before, after in stages:
        groups = count // GROUP
        before(first_row, GROUP, slots[turn])
        if waiting is not None:
            waiting()

        def body(h, carry, first_row=first_row, before=before, after=after, turn=turn):
            row0 = first_row + h * (2 * GROUP)
            before(row0 + GROUP, GROUP, slots[1 - turn])
            after(row0, GROUP, slots[turn])
            before(row0 + 2 * GROUP, GROUP, slots[turn])
            after(row0 + GROUP, GROUP, slots[1 - turn])
            return carry

        loops = (groups - 1) // 2
        if loops > 2:
            if before is grid_part:
                prepare(0, height)
            lax.fori_loop(0, loops, body, 0)
        else:
            for h in range(loops):
                body(h, 0)
        row0 = first_row + loops * (2 * GROUP)
        sizes = [GROUP] * ((groups - 1) % 2) + [count % GROUP] * (count % GROUP > 0)
        size = GROUP
        for following in sizes:
            before(row0 + size, following, slots[1 - turn])
            after(row0, size, slots[turn])
            row0, size, turn = row0 + size, following, 1 - turn
        waiting = functools.partial(after, row0, size, slots[turn])
        turn = 1 - turn
    waiting()
    for start in range(0, rows_tile, GROUP):
        sent(start).wait()


def project(count, f_ref, first_ref, second_ref, out_ref):
    weights = jnp.concatenate([first_ref[...], second_ref[...]], axis=0)
    mine = lax.dot_general(
        f_ref[...], weights, (((1,), (1,)), ((), ())), preferred_element_type=jnp.float32
    ).astype(jnp.bfloat16)
    out_ref[...] = jnp.broadcast_to(mine[None], (count,) + mine.shape)


def vmem_need(rows_tile, cols_tile, channels):
    height, width = rows_tile + 2 * MARGIN, cols_tile + 2 * MARGIN
    lanes = height * width
    cells = lanes * channels
    sums = 2 * 3 * channels * GROUP * width * 4
    grid = (height + 2) * 2 * channels * LANES * 2
    return cells * 4 + 3 * cells * 2 + sums + grid + channels * rows_tile * LANES * 2 + (6 << 20)


def call_trunk(rows_tile, cols_tile, bins, channels, *operands):
    vmem = pl.BlockSpec(memory_space=pltpu.VMEM)
    return pl.pallas_call(
        functools.partial(trunk, rows_tile, cols_tile, bins, channels),
        out_shape=jax.ShapeDtypeStruct((channels, rows_tile, cols_tile), jnp.bfloat16),
        in_specs=[pl.BlockSpec(memory_space=pltpu.SMEM)] + [vmem] * 6,
        out_specs=pl.BlockSpec(memory_space=pltpu.HBM),
        scratch_shapes=[
            pltpu.VMEM((channels, rows_tile, cols_tile), jnp.bfloat16),
            pltpu.SemaphoreType.DMA((rows_tile // GROUP,)),
        ],
        compiler_params=pltpu.CompilerParams(vmem_limit_bytes=vmem_need(rows_tile, cols_tile, channels)),
        name="trunk",
    )(*operands)


def local(
    features, first_weight, second_weight, conv_kernel, conv_bias, dilated_kernels, mixing_weights
):
    channels = first_weight.shape[1]
    row_count, col_count = lax.axis_size("row"), lax.axis_size("col")
    devices = row_count * col_count
    bins = features.shape[0] * devices
    vmem = pl.BlockSpec(memory_space=pltpu.VMEM)
    copies = pl.pallas_call(
        functools.partial(project, devices),
        out_shape=jax.ShapeDtypeStruct((devices, features.shape[0], 2 * channels), jnp.bfloat16),
        in_specs=[vmem] * 3,
        out_specs=vmem,
        compiler_params=pltpu.CompilerParams(vmem_limit_bytes=60 << 20),
        name="project",
    )(features, first_weight.T, second_weight.T)
    both = lax.all_to_all(copies, ("row", "col"), 0, 0).reshape(bins, 2 * channels)
    rows_tile = bins // row_count
    cols_tile = bins // col_count
    height, width = rows_tile + 2 * MARGIN, cols_tile + 2 * MARGIN
    row_start = lax.axis_index("row") * rows_tile
    col_start = lax.axis_index("col") * cols_tile
    pos = jnp.stack([row_start, col_start]).astype(jnp.int32)
    row_ids = row_start - MARGIN + jnp.arange(height, dtype=jnp.int32)
    col_ids = col_start - MARGIN + jnp.arange(width, dtype=jnp.int32)
    inside = ((row_ids >= 0) & (row_ids < bins))[:, None] & ((col_ids >= 0) & (col_ids < bins))[None]
    hi = jnp.where(inside, jnp.inf, FAR).astype(jnp.float32).reshape(1, height * width)
    straight = jnp.transpose(conv_kernel, (1, 2, 0, 3))
    swapped = jnp.transpose(conv_kernel, (0, 2, 1, 3))
    w1 = (0.5 * jnp.stack([straight, swapped], axis=3)).astype(jnp.bfloat16).reshape(3 * channels, 6 * channels)
    wd = jnp.transpose(dilated_kernels, (0, 2, 3, 1, 4)).reshape(3, 3 * channels, 3 * channels)
    return call_trunk(
        rows_tile, cols_tile, bins, channels, pos, both, w1, wd, mixing_weights, conv_bias[:, None], hi
    )


def solution(mesh):
    in_specs = (P(("groups", "row", "col"), None), P(), P(), P(), P(), P(), P())
    out_specs = P("groups", "row", "col")
    return jax.shard_map(local, mesh=mesh, in_specs=in_specs, out_specs=out_specs, check_vma=False)
```

```python
import functools

import jax
import jax.numpy as jnp
from jax import lax
from jax.experimental import pallas as pl
from jax.experimental.pallas import tpu as pltpu
from jax.sharding import PartitionSpec as P

MARGIN = 16
GROUP = 16
PITCH = GROUP + 1
LANES = 128
FAR = -1e30
SPREADS = (2, 4, 8)


def haloed(p_ref, start, count, bins):
    before = pl.multiple_of(jnp.maximum(start - MARGIN, 0), MARGIN)
    after = pl.multiple_of(jnp.minimum(start + count, bins - MARGIN), MARGIN)
    top = p_ref[pl.ds(before, MARGIN), :].astype(jnp.float32)
    mid = p_ref[pl.ds(pl.multiple_of(start, MARGIN), count), :].astype(jnp.float32)
    low = p_ref[pl.ds(after, MARGIN), :].astype(jnp.float32)
    top = jnp.where(start > 0, top, FAR)
    low = jnp.where(start + count < bins, low, FAR)
    return jnp.concatenate([top, mid, low], axis=0)


def trunk(
    rows_tile, cols_tile, bins, channels,
    pos_ref, p_ref, w1_ref, wd_ref, wm_ref, bias_ref, hi_ref, out_ref, staging, sems,
):
    height, width = rows_tile + 2 * MARGIN, cols_tile + 2 * MARGIN
    lanes = height * width
    both = 2 * channels
    z_shape = pltpu.VMEM((3 * channels, GROUP * width), jnp.float32)
    pl.run_scoped(
        functools.partial(
            staged, rows_tile, cols_tile, bins, channels,
            pos_ref, p_ref, w1_ref, wd_ref, wm_ref, bias_ref, hi_ref, out_ref, staging, sems,
        ),
        pltpu.VMEM((height + 2, both, LANES), jnp.bfloat16),
        pltpu.VMEM((both, 4 * width), jnp.bfloat16),
        pltpu.VMEM((channels, lanes), jnp.float32),
        pltpu.VMEM((channels, lanes), jnp.bfloat16),
        pltpu.VMEM((channels, lanes), jnp.bfloat16),
        pltpu.VMEM((channels, lanes), jnp.bfloat16),
        pltpu.VMEM((channels, LANES), jnp.bfloat16),
        pltpu.VMEM((channels * PITCH, LANES), jnp.float32),
        pltpu.VMEM((channels * PITCH, LANES), jnp.float32),
        z_shape,
        z_shape,
    )


def staged(
    rows_tile, cols_tile, bins, channels,
    pos_ref, p_ref, w1_ref, wd_ref, wm_ref, bias_ref, hi_ref, out_ref, staging, sems,
    rb, cpat, state, act_a, act_b, side, tail, flat_a, flat_b, z_a, z_b,
):
    width = cols_tile + 2 * MARGIN
    height = rows_tile + 2 * MARGIN
    period = 4 * width
    tiles = period // LANES
    both = 2 * channels
    zero = jnp.bfloat16(0)
    rows_t = jnp.transpose(haloed(p_ref, pos_ref[0], rows_tile, bins)).astype(jnp.bfloat16)
    cols_t = jnp.transpose(haloed(p_ref, pos_ref[1], cols_tile, bins))
    rb[0] = jnp.zeros((both, LANES), jnp.bfloat16)
    rb[height + 1] = jnp.zeros((both, LANES), jnp.bfloat16)
    ready = set()

    def prepare(start, stop):
        for i in range(max(start, 0), min(stop, height)):
            if i not in ready:
                ready.add(i)
                rb[i + 1] = jnp.broadcast_to(rows_t[:, i : i + 1], (both, LANES))

    cols_s = jnp.concatenate([cols_t[channels:], cols_t[:channels]], axis=0)
    cpat[...] = jnp.concatenate([cols_s] * 4, axis=1).astype(jnp.bfloat16)
    tail[...] = jnp.zeros_like(tail)

    lane = lax.broadcasted_iota(jnp.int32, (both, LANES), 1)

    def at(row0, rows, shift=0):
        start = row0 * width + shift
        return pl.ds(start if isinstance(start, int) else pl.multiple_of(start, LANES), rows * width)

    def gathered(z_ref, rows, spread):
        size = rows * width
        return (
            z_ref[channels : 2 * channels, :size]
            + pltpu.roll(z_ref[:channels, :size], spread, axis=1)
            + pltpu.roll(z_ref[2 * channels :, :size], size - spread, axis=1)
        )

    def grid_part(row0, rows, z_ref):
        size = rows * width
        if isinstance(row0, int):
            prepare(row0 - 1, row0 + rows + 1)
        for pair in range(size // (2 * LANES)):
            halves = []
            for t in (2 * pair, 2 * pair + 1):
                base = 4 * (t // tiles)
                t = t % tiles
                r0 = (t * LANES) // width
                r1 = (t * LANES + LANES - 1) // width
                split = r1 * width - t * LANES
                col = cpat[:, t * LANES : (t + 1) * LANES]
                pieces = []
                for p in (-1, 0, 1):
                    row = rb[row0 + (base + r0 + p + 1)]
                    if r1 != r0:
                        row = jnp.where(lane < split, row, rb[row0 + (base + r1 + p + 1)])
                    pieces.append(jnp.maximum(row + col, zero))
                halves.append(jnp.concatenate(pieces, axis=0))
            x = jnp.concatenate(halves, axis=1)
            z_ref[:, pair * 2 * LANES : (pair + 1) * 2 * LANES] = jnp.dot(
                w1_ref[...], x, preferred_element_type=jnp.float32
            )

    def start_part(row0, rows, z_ref):
        size = rows * width
        st = jnp.minimum(gathered(z_ref, rows, 1) + bias_ref[...], hi_ref[:, at(row0, rows)])
        act = jnp.maximum(st.astype(jnp.bfloat16), zero)
        window = jnp.concatenate([tail[...], act], axis=1)
        tail[...] = act[:, size - LANES :]
        state[:, at(row0, rows)] = st
        act_a[:, at(row0, rows)] = act
        side[:, at(row0, rows)] = window[:, LANES // 2 : LANES // 2 + size]

    pending = []

    def flush():
        while pending:
            pending.pop()()

    stages = [(0, height, grid_part, start_part)]
    src, dst = act_a, act_b
    for block, spread in enumerate(SPREADS):
        shift = spread * width
        ragged = shift % LANES
        assert ragged in (0, LANES // 2)
        edge = 4 if spread == 2 else 2 * spread
        last = block == len(SPREADS) - 1
        around = side if ragged else src

        def conv_part(row0, rows, z_ref, block=block, shift=shift, ragged=ragged, src=src, around=around):
            x = jnp.concatenate(
                [
                    around[:, at(row0, rows, ragged - shift)],
                    src[:, at(row0, rows)],
                    around[:, at(row0, rows, ragged + shift)],
                ],
                axis=0,
            )
            z_ref[:, : rows * width] = jnp.dot(wd_ref[block], x, preferred_element_type=jnp.float32)

        def mix_part(row0, rows, z_ref, block=block, spread=spread, dst=dst, last=last):
            gated = jnp.maximum(gathered(z_ref, rows, spread).astype(jnp.bfloat16), zero)
            if last:
                flush()
            st = state[:, at(row0, rows)] + jnp.dot(wm_ref[block], gated, preferred_element_type=jnp.float32)
            flat = flat_a if z_ref is z_a else flat_b
            if not last:
                state[:, at(row0, rows)] = st
                dst[:, at(row0, rows)] = jnp.maximum(st.astype(jnp.bfloat16), zero)
                return None
            result = st.astype(jnp.bfloat16)

            def send():
                for k in range(rows):
                    row = result[:, k * width + MARGIN : k * width + MARGIN + LANES]
                    flat[pl.ds(k, channels, stride=PITCH), :] = row.astype(jnp.float32)
                start = row0 - MARGIN
                place = pl.ds(start if isinstance(start, int) else pl.multiple_of(start, GROUP), GROUP)
                for c in range(channels):
                    staging[c, place, :] = flat[c * PITCH : c * PITCH + GROUP, :].astype(jnp.bfloat16)
                sent(start).start()

            return send

        stages.append((edge, height - 2 * edge, conv_part, mix_part))
        src, dst = dst, src

    def sent(start):
        place = pl.ds(start if isinstance(start, int) else pl.multiple_of(start, GROUP), GROUP)
        return pltpu.make_async_copy(staging.at[:, place, :], out_ref.at[:, place, :], sems.at[start // GROUP])

    slots = (z_a, z_b)
    def run(after, *place):
        send = after(*place)
        if send is not None:
            pending.append(send)

    waiting = None
    turn = 0
    for first_row, count, before, after in stages:
        groups = count // GROUP
        before(first_row, GROUP, slots[turn])
        if waiting is not None:
            waiting()

        def body(h, carry, first_row=first_row, before=before, after=after, turn=turn):
            row0 = first_row + h * (2 * GROUP)
            before(row0 + GROUP, GROUP, slots[1 - turn])
            run(after, row0, GROUP, slots[turn])
            before(row0 + 2 * GROUP, GROUP, slots[turn])
            run(after, row0 + GROUP, GROUP, slots[1 - turn])
            return carry

        loops = (groups - 1) // 2
        if loops > 2:
            if before is grid_part:
                prepare(0, height)

            def closed(h, carry, body=body):
                body(h, carry)
                flush()
                return carry

            lax.fori_loop(0, loops, closed, 0)
        else:
            for h in range(loops):
                body(h, 0)
        row0 = first_row + loops * (2 * GROUP)
        sizes = [GROUP] * ((groups - 1) % 2) + [count % GROUP] * (count % GROUP > 0)
        size = GROUP
        for following in sizes:
            before(row0 + size, following, slots[1 - turn])
            run(after, row0, size, slots[turn])
            row0, size, turn = row0 + size, following, 1 - turn
        waiting = functools.partial(run, after, row0, size, slots[turn])
        turn = 1 - turn
    waiting()
    flush()
    for start in range(0, rows_tile, GROUP):
        sent(start).wait()


def project(count, f_ref, first_ref, second_ref, out_ref):
    weights = jnp.concatenate([first_ref[...], second_ref[...]], axis=0)
    mine = lax.dot_general(
        f_ref[...], weights, (((1,), (1,)), ((), ())), preferred_element_type=jnp.float32
    ).astype(jnp.bfloat16)
    out_ref[...] = jnp.broadcast_to(mine[None], (count,) + mine.shape)


def vmem_need(rows_tile, cols_tile, channels):
    height, width = rows_tile + 2 * MARGIN, cols_tile + 2 * MARGIN
    lanes = height * width
    cells = lanes * channels
    sums = 2 * 3 * channels * GROUP * width * 4
    grid = (height + 2) * 2 * channels * LANES * 2
    return cells * 4 + 3 * cells * 2 + sums + grid + channels * rows_tile * LANES * 2 + (6 << 20)


def call_trunk(rows_tile, cols_tile, bins, channels, *operands):
    vmem = pl.BlockSpec(memory_space=pltpu.VMEM)
    return pl.pallas_call(
        functools.partial(trunk, rows_tile, cols_tile, bins, channels),
        out_shape=jax.ShapeDtypeStruct((channels, rows_tile, cols_tile), jnp.bfloat16),
        in_specs=[pl.BlockSpec(memory_space=pltpu.SMEM)] + [vmem] * 6,
        out_specs=pl.BlockSpec(memory_space=pltpu.HBM),
        scratch_shapes=[
            pltpu.VMEM((channels, rows_tile, cols_tile), jnp.bfloat16),
            pltpu.SemaphoreType.DMA((rows_tile // GROUP,)),
        ],
        compiler_params=pltpu.CompilerParams(vmem_limit_bytes=vmem_need(rows_tile, cols_tile, channels)),
        name="trunk",
    )(*operands)


def local(
    features, first_weight, second_weight, conv_kernel, conv_bias, dilated_kernels, mixing_weights
):
    channels = first_weight.shape[1]
    row_count, col_count = lax.axis_size("row"), lax.axis_size("col")
    devices = row_count * col_count
    bins = features.shape[0] * devices
    vmem = pl.BlockSpec(memory_space=pltpu.VMEM)
    copies = pl.pallas_call(
        functools.partial(project, devices),
        out_shape=jax.ShapeDtypeStruct((devices, features.shape[0], 2 * channels), jnp.bfloat16),
        in_specs=[vmem] * 3,
        out_specs=vmem,
        compiler_params=pltpu.CompilerParams(vmem_limit_bytes=60 << 20),
        name="project",
    )(features, first_weight.T, second_weight.T)
    both = lax.all_to_all(copies, ("row", "col"), 0, 0).reshape(bins, 2 * channels)
    rows_tile = bins // row_count
    cols_tile = bins // col_count
    height, width = rows_tile + 2 * MARGIN, cols_tile + 2 * MARGIN
    row_start = lax.axis_index("row") * rows_tile
    col_start = lax.axis_index("col") * cols_tile
    pos = jnp.stack([row_start, col_start]).astype(jnp.int32)
    row_ids = row_start - MARGIN + jnp.arange(height, dtype=jnp.int32)
    col_ids = col_start - MARGIN + jnp.arange(width, dtype=jnp.int32)
    inside = ((row_ids >= 0) & (row_ids < bins))[:, None] & ((col_ids >= 0) & (col_ids < bins))[None]
    hi = jnp.where(inside, jnp.inf, FAR).astype(jnp.float32).reshape(1, height * width)
    straight = jnp.transpose(conv_kernel, (1, 2, 0, 3))
    swapped = jnp.transpose(conv_kernel, (0, 2, 1, 3))
    w1 = (0.5 * jnp.stack([straight, swapped], axis=3)).astype(jnp.bfloat16).reshape(3 * channels, 6 * channels)
    wd = jnp.transpose(dilated_kernels, (0, 2, 3, 1, 4)).reshape(3, 3 * channels, 3 * channels)
    return call_trunk(
        rows_tile, cols_tile, bins, channels, pos, both, w1, wd, mixing_weights, conv_bias[:, None], hi
    )


def solution(mesh):
    in_specs = (P(("groups", "row", "col"), None), P(), P(), P(), P(), P(), P())
    out_specs = P("groups", "row", "col")
    return jax.shard_map(local, mesh=mesh, in_specs=in_specs, out_specs=out_specs, check_vma=False)
```

```python
import functools

import jax
import jax.numpy as jnp
from jax import lax
from jax.experimental import pallas as pl
from jax.experimental.pallas import tpu as pltpu
from jax.sharding import PartitionSpec as P

MARGIN = 16
GROUP = 16
PITCH = GROUP + 1
LANES = 128
FAR = -1e30
SPREADS = (2, 4, 8)


def haloed(p_ref, start, count, bins):
    before = pl.multiple_of(jnp.maximum(start - MARGIN, 0), MARGIN)
    after = pl.multiple_of(jnp.minimum(start + count, bins - MARGIN), MARGIN)
    top = p_ref[pl.ds(before, MARGIN), :].astype(jnp.float32)
    mid = p_ref[pl.ds(pl.multiple_of(start, MARGIN), count), :].astype(jnp.float32)
    low = p_ref[pl.ds(after, MARGIN), :].astype(jnp.float32)
    top = jnp.where(start > 0, top, FAR)
    low = jnp.where(start + count < bins, low, FAR)
    return jnp.concatenate([top, mid, low], axis=0)


def trunk(
    rows_tile, cols_tile, bins, channels,
    pos_ref, p_ref, w1_ref, wd_ref, wm_ref, bias_ref, hi_ref, out_ref, staging, sems,
):
    height, width = rows_tile + 2 * MARGIN, cols_tile + 2 * MARGIN
    lanes = height * width
    both = 2 * channels
    z_shape = pltpu.VMEM((3 * channels, GROUP * width), jnp.float32)
    pl.run_scoped(
        functools.partial(
            staged, rows_tile, cols_tile, bins, channels,
            pos_ref, p_ref, w1_ref, wd_ref, wm_ref, bias_ref, hi_ref, out_ref, staging, sems,
        ),
        pltpu.VMEM((height + 2, both, LANES), jnp.bfloat16),
        pltpu.VMEM((both, 4 * width), jnp.bfloat16),
        pltpu.VMEM((channels, lanes), jnp.float32),
        pltpu.VMEM((channels, lanes), jnp.bfloat16),
        pltpu.VMEM((channels, lanes), jnp.bfloat16),
        pltpu.VMEM((channels, lanes), jnp.bfloat16),
        pltpu.VMEM((channels, LANES), jnp.bfloat16),
        pltpu.VMEM(((channels + 1) * PITCH, LANES), jnp.float32),
        pltpu.VMEM(((channels + 1) * PITCH, LANES), jnp.float32),
        z_shape,
        z_shape,
    )


def staged(
    rows_tile, cols_tile, bins, channels,
    pos_ref, p_ref, w1_ref, wd_ref, wm_ref, bias_ref, hi_ref, out_ref, staging, sems,
    rb, cpat, state, act_a, act_b, side, tail, flat_a, flat_b, z_a, z_b,
):
    width = cols_tile + 2 * MARGIN
    height = rows_tile + 2 * MARGIN
    period = 4 * width
    tiles = period // LANES
    both = 2 * channels
    zero = jnp.bfloat16(0)
    rows_t = jnp.transpose(haloed(p_ref, pos_ref[0], rows_tile, bins)).astype(jnp.bfloat16)
    cols_t = jnp.transpose(haloed(p_ref, pos_ref[1], cols_tile, bins))
    rb[0] = jnp.zeros((both, LANES), jnp.bfloat16)
    rb[height + 1] = jnp.zeros((both, LANES), jnp.bfloat16)
    ready = set()

    def prepare(start, stop):
        for i in range(max(start, 0), min(stop, height)):
            if i not in ready:
                ready.add(i)
                rb[i + 1] = jnp.broadcast_to(rows_t[:, i : i + 1], (both, LANES))

    cols_s = jnp.concatenate([cols_t[channels:], cols_t[:channels]], axis=0)
    cpat[...] = jnp.concatenate([cols_s] * 4, axis=1).astype(jnp.bfloat16)
    tail[...] = jnp.zeros_like(tail)

    lane = lax.broadcasted_iota(jnp.int32, (both, LANES), 1)

    def at(row0, rows, shift=0):
        start = row0 * width + shift
        return pl.ds(start if isinstance(start, int) else pl.multiple_of(start, LANES), rows * width)

    def gathered(z_ref, rows, spread):
        size = rows * width
        return (
            z_ref[channels : 2 * channels, :size]
            + pltpu.roll(z_ref[:channels, :size], spread, axis=1)
            + pltpu.roll(z_ref[2 * channels :, :size], size - spread, axis=1)
        )

    def grid_part(row0, rows, z_ref):
        size = rows * width
        if isinstance(row0, int):
            prepare(row0 - 1, row0 + rows + 1)
        for pair in range(size // (2 * LANES)):
            halves = []
            for t in (2 * pair, 2 * pair + 1):
                base = 4 * (t // tiles)
                t = t % tiles
                r0 = (t * LANES) // width
                r1 = (t * LANES + LANES - 1) // width
                split = r1 * width - t * LANES
                col = cpat[:, t * LANES : (t + 1) * LANES]
                pieces = []
                for p in (-1, 0, 1):
                    row = rb[row0 + (base + r0 + p + 1)]
                    if r1 != r0:
                        row = jnp.where(lane < split, row, rb[row0 + (base + r1 + p + 1)])
                    pieces.append(jnp.maximum(row + col, zero))
                halves.append(jnp.concatenate(pieces, axis=0))
            x = jnp.concatenate(halves, axis=1)
            z_ref[:, pair * 2 * LANES : (pair + 1) * 2 * LANES] = jnp.dot(
                w1_ref[...], x, preferred_element_type=jnp.float32
            )

    def start_part(row0, rows, z_ref):
        size = rows * width
        st = jnp.minimum(gathered(z_ref, rows, 1) + bias_ref[...], hi_ref[:, at(row0, rows)])
        act = jnp.maximum(st.astype(jnp.bfloat16), zero)
        window = jnp.concatenate([tail[...], act], axis=1)
        tail[...] = act[:, size - LANES :]
        state[:, at(row0, rows)] = st
        act_a[:, at(row0, rows)] = act
        side[:, at(row0, rows)] = window[:, LANES // 2 : LANES // 2 + size]

    pending = []

    def flush():
        while pending:
            pending.pop()()

    stages = [(0, height, grid_part, start_part)]
    src, dst = act_a, act_b
    for block, spread in enumerate(SPREADS):
        shift = spread * width
        ragged = shift % LANES
        assert ragged in (0, LANES // 2)
        edge = 4 if spread == 2 else 2 * spread
        last = block == len(SPREADS) - 1
        around = side if ragged else src

        def conv_part(row0, rows, z_ref, block=block, shift=shift, ragged=ragged, src=src, around=around):
            x = jnp.concatenate(
                [
                    around[:, at(row0, rows, ragged - shift)],
                    src[:, at(row0, rows)],
                    around[:, at(row0, rows, ragged + shift)],
                ],
                axis=0,
            )
            z_ref[:, : rows * width] = jnp.dot(wd_ref[block], x, preferred_element_type=jnp.float32)

        def mix_part(row0, rows, z_ref, block=block, spread=spread, dst=dst, last=last):
            gated = jnp.maximum(gathered(z_ref, rows, spread).astype(jnp.bfloat16), zero)
            if last:
                flush()
            st = state[:, at(row0, rows)] + jnp.dot(wm_ref[block], gated, preferred_element_type=jnp.float32)
            flat = flat_a if z_ref is z_a else flat_b
            if not last:
                state[:, at(row0, rows)] = st
                dst[:, at(row0, rows)] = jnp.maximum(st.astype(jnp.bfloat16), zero)
                return None
            result = st.astype(jnp.bfloat16)

            def send():
                for k in range(rows):
                    row = result[:, k * width + MARGIN : k * width + MARGIN + LANES]
                    flat[pl.ds(k, channels, stride=PITCH), :] = row.astype(jnp.float32)
                start = row0 - MARGIN
                place = pl.ds(start if isinstance(start, int) else pl.multiple_of(start, GROUP), GROUP)
                for c in range(channels):
                    staging[c, place, :] = flat[c * PITCH : c * PITCH + GROUP, :].astype(jnp.bfloat16)
                sent(start).start()

            return send

        stages.append((edge, height - 2 * edge, conv_part, mix_part))
        src, dst = dst, src

    def sent(start):
        place = pl.ds(start if isinstance(start, int) else pl.multiple_of(start, GROUP), GROUP)
        return pltpu.make_async_copy(staging.at[:, place, :], out_ref.at[:, place, :], sems.at[start // GROUP])

    slots = (z_a, z_b)
    def run(after, *place):
        send = after(*place)
        if send is not None:
            pending.append(send)

    waiting = None
    turn = 0
    for first_row, count, before, after in stages:
        groups = count // GROUP
        before(first_row, GROUP, slots[turn])
        if waiting is not None:
            waiting()

        def body(h, carry, first_row=first_row, before=before, after=after, turn=turn):
            row0 = first_row + h * (2 * GROUP)
            before(row0 + GROUP, GROUP, slots[1 - turn])
            run(after, row0, GROUP, slots[turn])
            before(row0 + 2 * GROUP, GROUP, slots[turn])
            run(after, row0 + GROUP, GROUP, slots[1 - turn])
            return carry

        loops = (groups - 1) // 2
        if loops > 2:
            if before is grid_part:
                prepare(0, height)

            def closed(h, carry, body=body):
                body(h, carry)
                flush()
                return carry

            lax.fori_loop(0, loops, closed, 0)
        else:
            for h in range(loops):
                body(h, 0)
        row0 = first_row + loops * (2 * GROUP)
        sizes = [GROUP] * ((groups - 1) % 2) + [count % GROUP] * (count % GROUP > 0)
        size = GROUP
        for following in sizes:
            before(row0 + size, following, slots[1 - turn])
            run(after, row0, size, slots[turn])
            row0, size, turn = row0 + size, following, 1 - turn
        waiting = functools.partial(run, after, row0, size, slots[turn])
        turn = 1 - turn
    waiting()
    flush()
    for start in range(0, rows_tile, GROUP):
        sent(start).wait()


def project(count, f_ref, first_ref, second_ref, out_ref):
    weights = jnp.concatenate([first_ref[...], second_ref[...]], axis=0)
    mine = lax.dot_general(
        f_ref[...], weights, (((1,), (1,)), ((), ())), preferred_element_type=jnp.float32
    ).astype(jnp.bfloat16)
    out_ref[...] = jnp.broadcast_to(mine[None], (count,) + mine.shape)


def vmem_need(rows_tile, cols_tile, channels):
    height, width = rows_tile + 2 * MARGIN, cols_tile + 2 * MARGIN
    lanes = height * width
    cells = lanes * channels
    sums = 2 * 3 * channels * GROUP * width * 4
    grid = (height + 2) * 2 * channels * LANES * 2
    return cells * 4 + 3 * cells * 2 + sums + grid + channels * rows_tile * LANES * 2 + (6 << 20)


def call_trunk(rows_tile, cols_tile, bins, channels, *operands):
    vmem = pl.BlockSpec(memory_space=pltpu.VMEM)
    return pl.pallas_call(
        functools.partial(trunk, rows_tile, cols_tile, bins, channels),
        out_shape=jax.ShapeDtypeStruct((channels, rows_tile, cols_tile), jnp.bfloat16),
        in_specs=[pl.BlockSpec(memory_space=pltpu.SMEM)] + [vmem] * 6,
        out_specs=pl.BlockSpec(memory_space=pltpu.HBM),
        scratch_shapes=[
            pltpu.VMEM((channels, rows_tile, cols_tile), jnp.bfloat16),
            pltpu.SemaphoreType.DMA((rows_tile // GROUP,)),
        ],
        compiler_params=pltpu.CompilerParams(vmem_limit_bytes=vmem_need(rows_tile, cols_tile, channels)),
        name="trunk",
    )(*operands)


def local(
    features, first_weight, second_weight, conv_kernel, conv_bias, dilated_kernels, mixing_weights
):
    channels = first_weight.shape[1]
    row_count, col_count = lax.axis_size("row"), lax.axis_size("col")
    devices = row_count * col_count
    bins = features.shape[0] * devices
    vmem = pl.BlockSpec(memory_space=pltpu.VMEM)
    copies = pl.pallas_call(
        functools.partial(project, devices),
        out_shape=jax.ShapeDtypeStruct((devices, features.shape[0], 2 * channels), jnp.bfloat16),
        in_specs=[vmem] * 3,
        out_specs=vmem,
        compiler_params=pltpu.CompilerParams(vmem_limit_bytes=60 << 20),
        name="project",
    )(features, first_weight.T, second_weight.T)
    both = lax.all_to_all(copies, ("row", "col"), 0, 0).reshape(bins, 2 * channels)
    rows_tile = bins // row_count
    cols_tile = bins // col_count
    height, width = rows_tile + 2 * MARGIN, cols_tile + 2 * MARGIN
    row_start = lax.axis_index("row") * rows_tile
    col_start = lax.axis_index("col") * cols_tile
    pos = jnp.stack([row_start, col_start]).astype(jnp.int32)
    row_ids = row_start - MARGIN + jnp.arange(height, dtype=jnp.int32)
    col_ids = col_start - MARGIN + jnp.arange(width, dtype=jnp.int32)
    inside = ((row_ids >= 0) & (row_ids < bins))[:, None] & ((col_ids >= 0) & (col_ids < bins))[None]
    hi = jnp.where(inside, jnp.inf, FAR).astype(jnp.float32).reshape(1, height * width)
    straight = jnp.transpose(conv_kernel, (1, 2, 0, 3))
    swapped = jnp.transpose(conv_kernel, (0, 2, 1, 3))
    w1 = (0.5 * jnp.stack([straight, swapped], axis=3)).astype(jnp.bfloat16).reshape(3 * channels, 6 * channels)
    wd = jnp.transpose(dilated_kernels, (0, 2, 3, 1, 4)).reshape(3, 3 * channels, 3 * channels)
    return call_trunk(
        rows_tile, cols_tile, bins, channels, pos, both, w1, wd, mixing_weights, conv_bias[:, None], hi
    )


def solution(mesh):
    in_specs = (P(("groups", "row", "col"), None), P(), P(), P(), P(), P(), P())
    out_specs = P("groups", "row", "col")
    return jax.shard_map(local, mesh=mesh, in_specs=in_specs, out_specs=out_specs, check_vma=False)
```
